32 devices in a mesh: row: 2 (over core), col: 16 (over z, y, x).
Axes of the slice: x: 2, y: 2, z: 4, core: 2. Of those that a mesh axis runs over, the one named last changes fastest.
Arguments:
- mat_a: bfloat16 [5120, 24576], P('row', 'col'), may hold values from -6 to 6
- mat_b: bfloat16 [24576, 4096], P('row', 'col'), may hold values from -0.15625 to 0.15625
- mask_a: int32 [40, 192], P('row', 'col'), may hold values from 0 to 1, as said below
- mask_b: int32 [192, 32], P('row', 'col'), may hold values 0 or 1
Outputs:
- product: bfloat16 [5120, 4096], P('row', 'col')
The draws below stay inside these ranges and needn't reach their ends.
Inputs may be any that keep to these rules, and one draw needn't show every extreme that they name: `mask_a`: in each tile of 20 x 12 entries, the block rows holding an occupied block come first and each holds at least one; in every draw some tile has all 20 block rows occupied.
All inputs are finite; a program needn't handle non-finite values. No bound on the sum of `mask_b` on one device may be relied on, other than what follows from the above.
Results may differ from the reference program's by a relative error of at most 0.0025.
Values may be sent and summed in bfloat16 or wider, within the bound.
A program may use at most 128 MiB of HBM per device.

```python
import jax
import jax.numpy as jnp
from jax import lax

BLK = 128
RB = 20
KB = 12
CB = 2
SLOTS = 8
ROWS = 5120
INNER = 24576
COLS = 4096
N_ROW = 2
N_COL = 16


def draw_mask_a(key, part):
    keys = jax.random.split(jax.random.fold_in(key, 11), 5)
    heavy = jax.random.randint(keys[0], (N_ROW, N_COL), 0, 4) == 0
    light = jax.random.randint(keys[1], (N_ROW, N_COL), 1, min(4, RB) + 1)
    counts = jnp.where(heavy, RB, light)
    chosen = jax.random.randint(keys[2], (), 0, N_ROW * N_COL)
    places = jnp.arange(N_ROW * N_COL).reshape(N_ROW, N_COL)
    counts = jnp.where(places == chosen, RB, counts)
    blocks = jax.random.randint(keys[3], (N_ROW, RB, N_COL, KB), 0, 4) != 0
    needed = jax.random.randint(keys[4], (N_ROW, RB, N_COL, 1), 0, KB)
    blocks = jnp.logical_or(blocks, jnp.arange(KB)[None, None, None, :] == needed)
    living = jnp.arange(RB)[None, :, None, None] < counts[:, None, :, None]
    occupied = jnp.logical_and(blocks, living).astype(jnp.int32)
    return occupied.reshape(N_ROW * RB, N_COL * KB)


def touch_ends(drawn, own_key, smallest, high):
    longest = drawn.shape.index(max(drawn.shape))
    spots = []
    for shift in (0, 1):
        where = [jax.random.randint(jax.random.fold_in(own_key, axis), (), 0, length) for axis, length in enumerate(drawn.shape)]
        where[longest] = (where[longest] + shift) % drawn.shape[longest]
        spots.append(tuple(where))
    return drawn.at[spots[0]].set(smallest).at[spots[1]].set(high)


def steps_of(stream_key, shape, cuts, smallest, largest):
    def one(position, shards_of):
        heights = jax.random.uniform(jax.random.fold_in(jax.random.fold_in(stream_key, 6), position), (shards_of,), jnp.float32, smallest / len(cuts), largest / len(cuts))
        return jnp.repeat(jnp.exp(heights), shape[position] // shards_of).reshape((-1,) + (1,) * (len(shape) - position - 1))

    loudness = one(*cuts[0])
    for cut in cuts[1:]:
        loudness = loudness * one(*cut)
    return loudness


def gaussian(key, extent, scale, most, cuts=(), held_as=jnp.bfloat16):
    gain = steps_of(key, extent, cuts, -0.22, 0.18) if cuts else 1.0
    drawn = jax.random.normal(key, extent, jnp.float32) * scale * gain
    return jnp.minimum(jnp.maximum(drawn, -most), most).astype(held_as)


def setup_inputs(seed: int = 0) -> dict:
    splits = jax.random.split(jax.random.key(seed), 5)
    return {
        "mat_a": gaussian(splits[0], (ROWS, INNER), 1.0, 6.0, ((0, 2), (1, 16))),
        "mat_b": gaussian(splits[1], (INNER, COLS), (KB * BLK) ** -0.5, 0.15625, ((0, 2), (1, 16))),
        "mask_a": draw_mask_a(jax.random.fold_in(splits[4], 71), 0),
        "mask_b": touch_ends((jax.random.randint(splits[3], (N_COL * KB, N_COL * CB), 0, 4) < 3).astype(jnp.int32), jax.random.fold_in(splits[3], 1), 0, 1),
    }


def mask_blocks(matrix, occupied):
    rows, columns = occupied.shape
    blocked = matrix.reshape(rows, matrix.shape[0] // rows, columns, matrix.shape[1] // columns)
    scaling = occupied.astype(matrix.dtype)[:, None, :, None]
    return (blocked * scaling).reshape(matrix.shape)


def row_product(matrix_rows, right_tile, live_flags):
    stacked = matrix_rows.reshape(RB, BLK, matrix_rows.shape[1])

    def one_row(inputs):
        row_block, flagged = inputs
        return lax.cond(
            flagged,
            lambda piece: jnp.dot(piece, right_tile, preferred_element_type=jnp.float32),
            lambda piece: jnp.zeros((BLK, right_tile.shape[1]), jnp.float32),
            row_block,
        )

    return lax.map(one_row, (stacked, live_flags)).reshape(RB * BLK, right_tile.shape[1])


def reference(mat_a, mat_b, mask_a, mask_b):
    masked_a = mask_blocks(mat_a, mask_a)
    masked_b = mask_blocks(mat_b, mask_b)
    tiles_a = masked_a.reshape(N_ROW, RB * BLK, N_COL, KB * BLK).transpose(0, 2, 1, 3)
    stacked = masked_b.reshape(N_ROW, SLOTS, KB * BLK, N_COL, CB * BLK).transpose(0, 3, 1, 2, 4)
    first_b = stacked[:, :, 0]
    sent_b = jnp.concatenate([stacked[:1, :, 1], stacked[1:, :, 0]], axis=0)
    next_b = jnp.roll(sent_b, -1, axis=0)
    live_a = jnp.any(mask_a.reshape(N_ROW, RB, N_COL, KB) > 0, axis=3).transpose(0, 2, 1)
    next_a = jnp.roll(tiles_a, -1, axis=1)
    next_live = jnp.roll(live_a, -1, axis=1)
    count = N_ROW * N_COL
    inputs = (
        tiles_a.reshape(count, RB * BLK, KB * BLK),
        first_b.reshape(count, KB * BLK, CB * BLK),
        live_a.reshape(count, RB),
        next_a.reshape(count, RB * BLK, KB * BLK),
        next_b.reshape(count, KB * BLK, CB * BLK),
        next_live.reshape(count, RB),
    )

    def one_tile(pieces):
        first_a, first_right, first_live, second_a, second_right, second_live = pieces
        summed = row_product(first_a, first_right, first_live) + row_product(second_a, second_right, second_live)
        return summed.astype(jnp.bfloat16)

    result = lax.map(one_tile, inputs)
    result = result.reshape(N_ROW, N_COL, RB * BLK, CB * BLK).transpose(0, 2, 1, 3)
    return result.reshape(N_ROW * RB * BLK, N_COL * CB * BLK)
```

```python
import functools

import jax
import jax.numpy as jnp
from jax import lax
from jax.experimental import pallas as pl
from jax.experimental.pallas import tpu as pltpu
from jax.sharding import PartitionSpec as P

BLK = 128
LEVELS = 32767.0
TINY = 1e-33
MESH = pl.DeviceIdType.MESH


def times_flag(block, flag):
    scale = jnp.full(block.shape, flag.astype(jnp.float32)).astype(block.dtype)
    return block * scale


def kernel(
    group,
    a_hbm, b_hbm, flags_a, flags_b, out_ref,
    a_tile, b_own, b_raw, b_send, b_recv, own_sum, code_send, code_recv, step_send, step_recv,
    a_sem, b_sem, bs_sem, br_sem, cs_sem, cr_sem, ss_sem, sr_sem,
):
    n_row, n_col = lax.axis_size("row"), lax.axis_size("col")
    row, col = lax.axis_index("row"), lax.axis_index("col")
    up, down = lax.rem(row + n_row - 1, n_row), lax.rem(row + 1, n_row)
    left, right = lax.rem(col + n_col - 1, n_col), lax.rem(col + 1, n_col)
    rows, inner = a_tile.shape
    width = b_own.shape[1]
    deep, halves = inner // BLK, width // BLK
    span = group * BLK
    chunks = rows // span

    def piece(c):
        return pl.ds(pl.multiple_of(c * span, span), span)

    def load_a(c):
        return pltpu.make_async_copy(a_hbm.at[piece(c), :], a_tile.at[piece(c), :], a_sem.at[c])

    slot = jnp.where(row == 0, 1, 0)
    get_send = pltpu.make_async_copy(
        b_hbm.at[pl.ds(pl.multiple_of(slot * inner, inner), inner), :], b_raw, b_sem.at[0]
    )
    get_own = pltpu.make_async_copy(b_hbm.at[pl.ds(0, inner), :], b_own, b_sem.at[1])

    barrier = pltpu.get_barrier_semaphore()
    pl.semaphore_signal(barrier, inc=1, device_id={"row": down, "col": left}, device_id_type=MESH)
    pl.semaphore_signal(barrier, inc=1, device_id={"row": row, "col": right}, device_id_type=MESH)
    get_send.start()
    get_own.start()
    for c in range(chunks):
        load_a(c).start()

    get_send.wait()
    for h in range(halves):
        for k in range(deep):
            block = b_raw[k * BLK:(k + 1) * BLK, h * BLK:(h + 1) * BLK]
            b_send[h, k * BLK:(k + 1) * BLK, :] = times_flag(block, flags_b[slot * deep + k, h])

    def move_b(h):
        return pltpu.make_async_remote_copy(
            src_ref=b_send.at[h], dst_ref=b_recv.at[h], send_sem=bs_sem.at[h], recv_sem=br_sem.at[h],
            device_id={"row": up, "col": right}, device_id_type=MESH,
        )

    pl.semaphore_wait(barrier, 2)
    for h in range(halves):
        move_b(h).start()

    get_own.wait()
    for h in range(halves):
        for k in range(deep):
            spot = (slice(k * BLK, (k + 1) * BLK), slice(h * BLK, (h + 1) * BLK))
            b_own[spot] = times_flag(b_own[spot], flags_b[k, h])

    def own_part(c, carry):
        load_a(c).wait()
        for g in range(group):
            lines = pl.ds(pl.multiple_of(c * span + g * BLK, BLK), BLK)
            for k in range(deep):
                block = a_tile[lines, k * BLK:(k + 1) * BLK]
                a_tile[lines, k * BLK:(k + 1) * BLK] = times_flag(block, flags_a[c * group + g, k])
        own_sum[piece(c), :] = jnp.dot(a_tile[piece(c), :], b_own[...], preferred_element_type=jnp.float32)
        return carry

    lax.fori_loop(0, chunks, own_part, 0)

    def move_code(i):
        return pltpu.make_async_remote_copy(
            src_ref=code_send.at[i], dst_ref=code_recv.at[i], send_sem=cs_sem.at[i], recv_sem=cr_sem.at[i],
            device_id={"row": row, "col": left}, device_id_type=MESH,
        )

    def move_step(i):
        return pltpu.make_async_remote_copy(
            src_ref=step_send.at[i], dst_ref=step_recv.at[i], send_sem=ss_sem.at[i], recv_sem=sr_sem.at[i],
            device_id={"row": row, "col": left}, device_id_type=MESH,
        )

    for h in range(halves):
        move_b(h).wait_recv()

        def next_part(c, carry, h=h):
            i = h * chunks + c
            value = jnp.dot(a_tile[piece(c), :], b_recv[h], preferred_element_type=jnp.float32)
            most = jnp.maximum(jnp.max(jnp.abs(value), axis=0, keepdims=True), TINY)
            step_send[i] = jnp.broadcast_to(most * (1.0 / LEVELS), step_send.shape[1:])
            code_send[i] = jnp.round(value * (LEVELS / most)).astype(jnp.int32).astype(jnp.int16)
            move_step(i).start()
            move_code(i).start()
            return carry

        lax.fori_loop(0, chunks, next_part, 0)

    for h in range(halves):

        def finish(c, carry, h=h):
            i = h * chunks + c
            move_step(i).wait_recv()
            move_code(i).wait_recv()
            code = code_recv[i].astype(jnp.int32).astype(jnp.float32)
            total = own_sum[piece(c), h * BLK:(h + 1) * BLK] + code * step_recv[i, 0:1, :]
            out_ref[piece(c), h * BLK:(h + 1) * BLK] = total.astype(out_ref.dtype)
            return carry

        lax.fori_loop(0, chunks, finish, 0)

    for h in range(halves):
        move_b(h).wait_send()

    def sent(i, carry):
        move_step(i).wait_send()
        move_code(i).wait_send()
        return carry

    lax.fori_loop(0, halves * chunks, sent, 0)


def body(mat_a, mat_b, mask_a, mask_b):
    rows, inner = mat_a.shape
    width = mat_b.shape[1]
    block_rows = mask_a.shape[0]
    group = 2 if block_rows % 2 == 0 else 1
    span = group * BLK
    chunks = rows // span
    halves = width // BLK
    sends = halves * chunks
    dma = pltpu.SemaphoreType.DMA
    return pl.pallas_call(
        functools.partial(kernel, group),
        out_shape=jax.ShapeDtypeStruct((rows, width), jnp.bfloat16),
        in_specs=[
            pl.BlockSpec(memory_space=pl.ANY),
            pl.BlockSpec(memory_space=pl.ANY),
            pl.BlockSpec(memory_space=pltpu.SMEM),
            pl.BlockSpec(memory_space=pltpu.SMEM),
        ],
        out_specs=pl.BlockSpec(memory_space=pltpu.VMEM),
        scratch_shapes=[
            pltpu.VMEM((rows, inner), jnp.bfloat16),
            pltpu.VMEM((inner, width), jnp.bfloat16),
            pltpu.VMEM((inner, width), jnp.bfloat16),
            pltpu.VMEM((halves, inner, BLK), jnp.bfloat16),
            pltpu.VMEM((halves, inner, BLK), jnp.bfloat16),
            pltpu.VMEM((rows, width), jnp.float32),
            pltpu.VMEM((sends, span, BLK), jnp.int16),
            pltpu.VMEM((sends, span, BLK), jnp.int16),
            pltpu.VMEM((sends, 8, BLK), jnp.float32),
            pltpu.VMEM((sends, 8, BLK), jnp.float32),
            dma((chunks,)), dma((2,)), dma((halves,)), dma((halves,)),
            dma((sends,)), dma((sends,)), dma((sends,)), dma((sends,)),
        ],
        compiler_params=pltpu.CompilerParams(collective_id=0, has_side_effects=True),
        name="cannon",
    )(mat_a, mat_b, mask_a, mask_b)


def solution(mesh):
    return jax.shard_map(
        body,
        mesh=mesh,
        in_specs=(P("row", "col"), P("row", "col"), P("row", "col"), P("row", "col")),
        out_specs=P("row", "col"),
        check_vma=False,
    )
```

```python
import functools

import jax
import jax.numpy as jnp
from jax import lax
from jax.experimental import pallas as pl
from jax.experimental.pallas import tpu as pltpu
from jax.sharding import PartitionSpec as P

BLK = 128
LEVELS = 32767.0
TINY = 1e-33
MESH = pl.DeviceIdType.MESH


def times_flag(block, flag):
    scale = jnp.full(block.shape, flag.astype(jnp.float32)).astype(block.dtype)
    return block * scale


def kernel(
    group, parts,
    a_hbm, b_hbm, flags_a, flags_b, out_ref,
    a_tile, b_own, b_raw, b_send, b_recv, b_pass, own_sum, code_send, code_recv, step_send, step_recv,
    a_sem, b_sem, bs_sem, br_sem, ps_sem, pr_sem, cs_sem, cr_sem, ss_sem, sr_sem,
):
    n_row, n_col = lax.axis_size("row"), lax.axis_size("col")
    row, col = lax.axis_index("row"), lax.axis_index("col")
    up, down = lax.rem(row + n_row - 1, n_row), lax.rem(row + 1, n_row)
    left, right = lax.rem(col + n_col - 1, n_col), lax.rem(col + 1, n_col)
    rows, inner = a_tile.shape
    width = b_own.shape[1]
    deep, halves = inner // BLK, width // BLK
    span = group * BLK
    chunks = rows // span

    relayed = n_col % 4 == 0
    place = lax.rem(col, 4) if relayed else 0
    ahead = lax.rem(col + 2, n_col)
    behind = lax.rem(col + n_col - 2, n_col)
    depth = inner // parts

    def piece(c):
        return pl.ds(pl.multiple_of(c * span, span), span)

    def load_a(c):
        return pltpu.make_async_copy(a_hbm.at[piece(c), :], a_tile.at[piece(c), :], a_sem.at[c])

    slot = jnp.where(row == 0, 1, 0)
    get_send = pltpu.make_async_copy(
        b_hbm.at[pl.ds(pl.multiple_of(slot * inner, inner), inner), :], b_raw, b_sem.at[0]
    )
    get_own = pltpu.make_async_copy(b_hbm.at[pl.ds(0, inner), :], b_own, b_sem.at[1])

    barrier = pltpu.get_barrier_semaphore()
    if relayed:
        @pl.when(place == 2)
        def _():
            pl.semaphore_signal(barrier, inc=1, device_id={"row": row, "col": right}, device_id_type=MESH)

        @pl.when(place != 2)
        def _():
            pl.semaphore_signal(barrier, inc=1, device_id={"row": down, "col": left}, device_id_type=MESH)

        @pl.when(place == 3)
        def _():
            pl.semaphore_signal(barrier, inc=1, device_id={"row": down, "col": behind}, device_id_type=MESH)
    else:
        pl.semaphore_signal(barrier, inc=1, device_id={"row": down, "col": left}, device_id_type=MESH)
    pl.semaphore_signal(barrier, inc=1, device_id={"row": row, "col": right}, device_id_type=MESH)
    get_send.start()
    get_own.start()
    for c in range(chunks):
        load_a(c).start()

    get_send.wait()
    for h in range(halves):
        for k in range(deep):
            block = b_raw[k * BLK:(k + 1) * BLK, h * BLK:(h + 1) * BLK]
            b_send[h, k * BLK:(k + 1) * BLK, :] = times_flag(block, flags_b[h, slot * deep + k])

    def part(p):
        return pl.ds(pl.multiple_of(p * depth, depth), depth)

    def move_b(h, p):
        return pltpu.make_async_remote_copy(
            src_ref=b_send.at[h, part(p), :], dst_ref=b_recv.at[h, part(p), :],
            send_sem=bs_sem.at[h, p], recv_sem=br_sem.at[h, p],
            device_id={"row": up, "col": right}, device_id_type=MESH,
        )

    def hand_over(h, p):
        return pltpu.make_async_remote_copy(
            src_ref=b_send.at[h, part(p), :], dst_ref=b_pass.at[h, part(p), :],
            send_sem=bs_sem.at[h, p], recv_sem=pr_sem.at[h, p],
            device_id={"row": up, "col": ahead}, device_id_type=MESH,
        )

    def pass_on(h, p):
        return pltpu.make_async_remote_copy(
            src_ref=b_pass.at[h, part(p), :], dst_ref=b_recv.at[h, part(p), :],
            send_sem=ps_sem.at[h, p], recv_sem=br_sem.at[h, p],
            device_id={"row": row, "col": left}, device_id_type=MESH,
        )

    pl.semaphore_wait(barrier, jnp.where(place == 3, 3, 2) if relayed else 2)
    if relayed:
        @pl.when(place == 1)
        def _():
            for h in range(halves):
                for p in range(parts):
                    hand_over(h, p).start()

        @pl.when(place != 1)
        def _():
            for h in range(halves):
                for p in range(parts):
                    move_b(h, p).start()
    else:
        for h in range(halves):
            for p in range(parts):
                move_b(h, p).start()

    get_own.wait()
    for h in range(halves):
        for k in range(deep):
            spot = (slice(k * BLK, (k + 1) * BLK), slice(h * BLK, (h + 1) * BLK))
            b_own[spot] = times_flag(b_own[spot], flags_b[h, k])

    def own_part(c, carry):
        load_a(c).wait()
        if relayed:
            @pl.when((place == 3) & (lax.rem(c, 2) == 0) & (c >= 2) & (c < 2 * parts + 2))
            def _():
                p = c // 2 - 1
                hand_over(0, p).wait_recv()
                pass_on(0, p).start()

        for g in range(group):
            lines = pl.ds(pl.multiple_of(c * span + g * BLK, BLK), BLK)
            for k in range(deep):
                block = a_tile[lines, k * BLK:(k + 1) * BLK]
                a_tile[lines, k * BLK:(k + 1) * BLK] = times_flag(block, flags_a[k, c * group + g])
        own_sum[piece(c), :] = jnp.dot(a_tile[piece(c), :], b_own[...], preferred_element_type=jnp.float32)
        return carry

    lax.fori_loop(0, chunks, own_part, 0)

    def move_code(i):
        return pltpu.make_async_remote_copy(
            src_ref=code_send.at[i], dst_ref=code_recv.at[i], send_sem=cs_sem.at[i], recv_sem=cr_sem.at[i],
            device_id={"row": row, "col": left}, device_id_type=MESH,
        )

    def move_step(i):
        return pltpu.make_async_remote_copy(
            src_ref=step_send.at[i], dst_ref=step_recv.at[i], send_sem=ss_sem.at[i], recv_sem=sr_sem.at[i],
            device_id={"row": row, "col": left}, device_id_type=MESH,
        )

    for h in range(halves):
        if relayed and h > 0:
            @pl.when(place == 3)
            def _(h=h):
                for p in range(parts):
                    hand_over(h, p).wait_recv()
                    pass_on(h, p).start()

        for p in range(parts):
            move_b(h, p).wait_recv()

        def next_part(c, carry, h=h):
            i = h * chunks + c
            value = jnp.dot(a_tile[piece(c), :], b_recv[h], preferred_element_type=jnp.float32)
            most = jnp.maximum(jnp.max(jnp.abs(value), axis=0, keepdims=True), TINY)
            step_send[i] = jnp.broadcast_to(most * (1.0 / LEVELS), step_send.shape[1:])
            code_send[i] = jnp.round(value * (LEVELS / most)).astype(jnp.int32).astype(jnp.int16)
            move_step(i).start()
            move_code(i).start()
            return carry

        lax.fori_loop(0, chunks, next_part, 0)

    for h in range(halves):

        def finish(c, carry, h=h):
            i = h * chunks + c
            move_step(i).wait_recv()
            move_code(i).wait_recv()
            code = code_recv[i].astype(jnp.int32).astype(jnp.float32)
            total = own_sum[piece(c), h * BLK:(h + 1) * BLK] + code * step_recv[i, 0:1, :]
            out_ref[piece(c), h * BLK:(h + 1) * BLK] = total.astype(out_ref.dtype)
            return carry

        lax.fori_loop(0, chunks, finish, 0)

    for h in range(halves):
        for p in range(parts):
            move_b(h, p).wait_send()
    if relayed:
        @pl.when(place == 3)
        def _():
            for h in range(halves):
                for p in range(parts):
                    pass_on(h, p).wait_send()

    def sent(i, carry):
        move_step(i).wait_send()
        move_code(i).wait_send()
        return carry

    lax.fori_loop(0, halves * chunks, sent, 0)


def body(mat_a, mat_b, mask_a, mask_b):
    rows, inner = mat_a.shape
    width = mat_b.shape[1]
    block_rows = mask_a.shape[0]
    group = 2 if block_rows % 2 == 0 else 1
    span = group * BLK
    chunks = rows // span
    halves = width // BLK
    sends = halves * chunks
    parts = 4 if mask_a.shape[1] % 4 == 0 and chunks >= 10 else 1
    dma = pltpu.SemaphoreType.DMA
    return pl.pallas_call(
        functools.partial(kernel, group, parts),
        out_shape=jax.ShapeDtypeStruct((rows, width), jnp.bfloat16),
        in_specs=[
            pl.BlockSpec(memory_space=pl.ANY),
            pl.BlockSpec(memory_space=pl.ANY),
            pl.BlockSpec(memory_space=pltpu.SMEM),
            pl.BlockSpec(memory_space=pltpu.SMEM),
        ],
        out_specs=pl.BlockSpec(memory_space=pltpu.VMEM),
        scratch_shapes=[
            pltpu.VMEM((rows, inner), jnp.bfloat16),
            pltpu.VMEM((inner, width), jnp.bfloat16),
            pltpu.VMEM((inner, width), jnp.bfloat16),
            pltpu.VMEM((halves, inner, BLK), jnp.bfloat16),
            pltpu.VMEM((halves, inner, BLK), jnp.bfloat16),
            pltpu.VMEM((halves, inner, BLK), jnp.bfloat16),
            pltpu.VMEM((rows, width), jnp.float32),
            pltpu.VMEM((sends, span, BLK), jnp.int16),
            pltpu.VMEM((sends, span, BLK), jnp.int16),
            pltpu.VMEM((sends, 8, BLK), jnp.float32),
            pltpu.VMEM((sends, 8, BLK), jnp.float32),
            dma((chunks,)), dma((2,)), dma((halves, parts)), dma((halves, parts)),
            dma((halves, parts)), dma((halves, parts)),
            dma((sends,)), dma((sends,)), dma((sends,)), dma((sends,)),
        ],
        compiler_params=pltpu.CompilerParams(collective_id=0, has_side_effects=True),
        name="cannon",
    )(mat_a, mat_b, mask_a.T, mask_b.T)


def solution(mesh):
    return jax.shard_map(
        body,
        mesh=mesh,
        in_specs=(P("row", "col"), P("row", "col"), P("row", "col"), P("row", "col")),
        out_specs=P("row", "col"),
        check_vma=False,
    )
```

```python
import functools

import jax
import jax.numpy as jnp
from jax import lax
from jax.experimental import pallas as pl
from jax.experimental.pallas import tpu as pltpu
from jax.sharding import PartitionSpec as P

BLK = 128
LEVELS = 32767.0
TINY = 1e-33
MESH = pl.DeviceIdType.MESH


def times_flag(block, flag):
    scale = jnp.full(block.shape, flag.astype(jnp.float32)).astype(block.dtype)
    return block * scale


def kernel(
    group,
    a_hbm, b_hbm, flags_a, flags_b, out_ref,
    a_tile, b_own, b_raw, b_send, b_recv, own_sum, code_send, code_recv, step_send, step_recv,
    a_sem, b_sem, bs_sem, br_sem, cs_sem, cr_sem, ss_sem, sr_sem,
):
    n_row, n_col = lax.axis_size("row"), lax.axis_size("col")
    row, col = lax.axis_index("row"), lax.axis_index("col")
    up, down = lax.rem(row + n_row - 1, n_row), lax.rem(row + 1, n_row)
    left, right = lax.rem(col + n_col - 1, n_col), lax.rem(col + 1, n_col)
    rows, inner = a_tile.shape
    width = b_own.shape[1]
    deep, halves = inner // BLK, width // BLK
    span = group * BLK
    chunks = rows // span

    def piece(c):
        return pl.ds(pl.multiple_of(c * span, span), span)

    def load_a(c):
        return pltpu.make_async_copy(a_hbm.at[piece(c), :], a_tile.at[piece(c), :], a_sem.at[c])

    slot = jnp.where(row == 0, 1, 0)
    get_send = pltpu.make_async_copy(
        b_hbm.at[pl.ds(pl.multiple_of(slot * inner, inner), inner), :], b_raw, b_sem.at[0]
    )
    get_own = pltpu.make_async_copy(b_hbm.at[pl.ds(0, inner), :], b_own, b_sem.at[1])

    barrier = pltpu.get_barrier_semaphore()
    pl.semaphore_signal(barrier, inc=1, device_id={"row": down, "col": left}, device_id_type=MESH)
    pl.semaphore_signal(barrier, inc=1, device_id={"row": row, "col": right}, device_id_type=MESH)
    get_send.start()
    get_own.start()
    for c in range(chunks):
        load_a(c).start()

    get_send.wait()
    for h in range(halves):
        for k in range(deep):
            block = b_raw[k * BLK:(k + 1) * BLK, h * BLK:(h + 1) * BLK]
            b_send[h, k * BLK:(k + 1) * BLK, :] = times_flag(block, flags_b[h, slot * deep + k])

    def move_b(h):
        return pltpu.make_async_remote_copy(
            src_ref=b_send.at[h], dst_ref=b_recv.at[h], send_sem=bs_sem.at[h], recv_sem=br_sem.at[h],
            device_id={"row": up, "col": right}, device_id_type=MESH,
        )

    pl.semaphore_wait(barrier, 2)
    for h in range(halves):
        move_b(h).start()

    get_own.wait()
    for h in range(halves):
        for k in range(deep):
            spot = (slice(k * BLK, (k + 1) * BLK), slice(h * BLK, (h + 1) * BLK))
            b_own[spot] = times_flag(b_own[spot], flags_b[h, k])

    def own_part(c, carry):
        load_a(c).wait()
        for g in range(group):
            lines = pl.ds(pl.multiple_of(c * span + g * BLK, BLK), BLK)
            for k in range(deep):
                block = a_tile[lines, k * BLK:(k + 1) * BLK]
                a_tile[lines, k * BLK:(k + 1) * BLK] = times_flag(block, flags_a[k, c * group + g])
        own_sum[piece(c), :] = jnp.dot(a_tile[piece(c), :], b_own[...], preferred_element_type=jnp.float32)
        return carry

    lax.fori_loop(0, chunks, own_part, 0)

    def move_code(i):
        return pltpu.make_async_remote_copy(
            src_ref=code_send.at[i], dst_ref=code_recv.at[i], send_sem=cs_sem.at[i], recv_sem=cr_sem.at[i],
            device_id={"row": row, "col": left}, device_id_type=MESH,
        )

    def move_step(i):
        return pltpu.make_async_remote_copy(
            src_ref=step_send.at[i], dst_ref=step_recv.at[i], send_sem=ss_sem.at[i], recv_sem=sr_sem.at[i],
            device_id={"row": row, "col": left}, device_id_type=MESH,
        )

    def send_out(i, carry):
        move_step(i).start()
        move_code(i).start()
        return carry

    def next_part(h, early, c, carry):
        i = h * chunks + c
        value = jnp.dot(a_tile[piece(c), :], b_recv[h], preferred_element_type=jnp.float32)
        most = jnp.maximum(jnp.max(jnp.abs(value), axis=0, keepdims=True), TINY)
        step_send[i] = jnp.broadcast_to(most * (1.0 / LEVELS), step_send.shape[1:])
        code_send[i] = jnp.round(value * (LEVELS / most)).astype(jnp.int32).astype(jnp.int16)
        return carry if early else send_out(i, carry)

    for h in range(halves):
        move_b(h).wait_recv()
        if h == halves - 1:
            lax.fori_loop(0, h * chunks, send_out, 0)
        lax.fori_loop(0, chunks, functools.partial(next_part, h, h < halves - 1), 0)

    for h in range(halves):

        def finish(c, carry, h=h):
            i = h * chunks + c
            move_step(i).wait_recv()
            move_code(i).wait_recv()
            code = code_recv[i].astype(jnp.int32).astype(jnp.float32)
            total = own_sum[piece(c), h * BLK:(h + 1) * BLK] + code * step_recv[i, 0:1, :]
            out_ref[piece(c), h * BLK:(h + 1) * BLK] = total.astype(out_ref.dtype)
            return carry

        lax.fori_loop(0, chunks, finish, 0)

    for h in range(halves):
        move_b(h).wait_send()

    def sent(i, carry):
        move_step(i).wait_send()
        move_code(i).wait_send()
        return carry

    lax.fori_loop(0, halves * chunks, sent, 0)


def body(mat_a, mat_b, mask_a, mask_b):
    rows, inner = mat_a.shape
    width = mat_b.shape[1]
    block_rows = mask_a.shape[0]
    group = next(g for g in (4, 2, 1) if block_rows % g == 0)
    span = group * BLK
    chunks = rows // span
    halves = width // BLK
    sends = halves * chunks
    dma = pltpu.SemaphoreType.DMA
    return pl.pallas_call(
        functools.partial(kernel, group),
        out_shape=jax.ShapeDtypeStruct((rows, width), jnp.bfloat16),
        in_specs=[
            pl.BlockSpec(memory_space=pl.ANY),
            pl.BlockSpec(memory_space=pl.ANY),
            pl.BlockSpec(memory_space=pltpu.SMEM),
            pl.BlockSpec(memory_space=pltpu.SMEM),
        ],
        out_specs=pl.BlockSpec(memory_space=pltpu.VMEM),
        scratch_shapes=[
            pltpu.VMEM((rows, inner), jnp.bfloat16),
            pltpu.VMEM((inner, width), jnp.bfloat16),
            pltpu.VMEM((inner, width), jnp.bfloat16),
            pltpu.VMEM((halves, inner, BLK), jnp.bfloat16),
            pltpu.VMEM((halves, inner, BLK), jnp.bfloat16),
            pltpu.VMEM((rows, width), jnp.float32),
            pltpu.VMEM((sends, span, BLK), jnp.int16),
            pltpu.VMEM((sends, span, BLK), jnp.int16),
            pltpu.VMEM((sends, 8, BLK), jnp.float32),
            pltpu.VMEM((sends, 8, BLK), jnp.float32),
            dma((chunks,)), dma((2,)), dma((halves,)), dma((halves,)),
            dma((sends,)), dma((sends,)), dma((sends,)), dma((sends,)),
        ],
        compiler_params=pltpu.CompilerParams(collective_id=0, has_side_effects=True),
        name="cannon",
    )(mat_a, mat_b, mask_a.T, mask_b.T)


def solution(mesh):
    return jax.shard_map(
        body,
        mesh=mesh,
        in_specs=(P("row", "col"), P("row", "col"), P("row", "col"), P("row", "col")),
        out_specs=P("row", "col"),
        check_vma=False,
    )
```

```python
import functools

import jax
import jax.numpy as jnp
from jax import lax
from jax.experimental import pallas as pl
from jax.experimental.pallas import tpu as pltpu
from jax.sharding import PartitionSpec as P

BLK = 128
LEVELS = 32767.0
TINY = 1e-33
MESH = pl.DeviceIdType.MESH


def times_flag(block, flag):
    scale = jnp.full(block.shape, flag.astype(jnp.float32)).astype(block.dtype)
    return block * scale


def kernel(
    group,
    a_hbm, b_hbm, flags_a, flags_b, out_ref,
    a_tile, b_own, b_raw, b_send, b_recv, own_sum, code_send, code_recv, step_send, step_recv,
    a_sem, b_sem, bs_sem, br_sem, cs_sem, cr_sem, ss_sem, sr_sem,
):
    n_row, n_col = lax.axis_size("row"), lax.axis_size("col")
    row, col = lax.axis_index("row"), lax.axis_index("col")
    up, down = lax.rem(row + n_row - 1, n_row), lax.rem(row + 1, n_row)
    left, right = lax.rem(col + n_col - 1, n_col), lax.rem(col + 1, n_col)
    rows, inner = a_tile.shape
    width = b_own.shape[1]
    deep, halves = inner // BLK, width // BLK
    span = group * BLK
    chunks = rows // span

    def piece(c):
        return pl.ds(pl.multiple_of(c * span, span), span)

    def load_a(c):
        return pltpu.make_async_copy(a_hbm.at[piece(c), :], a_tile.at[piece(c), :], a_sem.at[c])

    slot = jnp.where(row == 0, 1, 0)
    get_send = pltpu.make_async_copy(
        b_hbm.at[pl.ds(pl.multiple_of(slot * inner, inner), inner), :], b_raw, b_sem.at[0]
    )
    get_own = pltpu.make_async_copy(b_hbm.at[pl.ds(0, inner), :], b_own, b_sem.at[1])

    barrier = pltpu.get_barrier_semaphore()
    pl.semaphore_signal(barrier, inc=1, device_id={"row": down, "col": left}, device_id_type=MESH)
    pl.semaphore_signal(barrier, inc=1, device_id={"row": row, "col": right}, device_id_type=MESH)
    get_send.start()
    get_own.start()
    for c in range(chunks):
        load_a(c).start()

    get_send.wait()
    for h in range(halves):
        for k in range(deep):
            block = b_raw[k * BLK:(k + 1) * BLK, h * BLK:(h + 1) * BLK]
            b_send[h, k * BLK:(k + 1) * BLK, :] = times_flag(block, flags_b[h, slot * deep + k])

    def move_b(h):
        return pltpu.make_async_remote_copy(
            src_ref=b_send.at[h], dst_ref=b_recv.at[h], send_sem=bs_sem.at[h], recv_sem=br_sem.at[h],
            device_id={"row": up, "col": right}, device_id_type=MESH,
        )

    pl.semaphore_wait(barrier, 2)
    for h in range(halves):
        move_b(h).start()

    get_own.wait()
    for h in range(halves):
        for k in range(deep):
            spot = (slice(k * BLK, (k + 1) * BLK), slice(h * BLK, (h + 1) * BLK))
            b_own[spot] = times_flag(b_own[spot], flags_b[h, k])

    def own_part(c, carry):
        load_a(c).wait()
        for g in range(group):
            lines = pl.ds(pl.multiple_of(c * span + g * BLK, BLK), BLK)
            for k in range(deep):
                block = a_tile[lines, k * BLK:(k + 1) * BLK]
                a_tile[lines, k * BLK:(k + 1) * BLK] = times_flag(block, flags_a[k, c * group + g])
        own_sum[piece(c), :] = jnp.dot(a_tile[piece(c), :], b_own[...], preferred_element_type=jnp.float32)
        return carry

    lax.fori_loop(0, chunks, own_part, 0)

    def move_code(i):
        return pltpu.make_async_remote_copy(
            src_ref=code_send.at[i], dst_ref=code_recv.at[i], send_sem=cs_sem.at[i], recv_sem=cr_sem.at[i],
            device_id={"row": row, "col": left}, device_id_type=MESH,
        )

    def move_step(i):
        return pltpu.make_async_remote_copy(
            src_ref=step_send.at[i], dst_ref=step_recv.at[i], send_sem=ss_sem.at[i], recv_sem=sr_sem.at[i],
            device_id={"row": row, "col": left}, device_id_type=MESH,
        )

    def send_out(i, carry):
        move_step(i).start()
        move_code(i).start()
        return carry

    def next_part(h, early, c, carry):
        i = h * chunks + c
        value = jnp.dot(a_tile[piece(c), :], b_recv[h], preferred_element_type=jnp.float32)
        most = jnp.maximum(jnp.max(jnp.abs(value), axis=0, keepdims=True), TINY)
        step_send[i] = jnp.broadcast_to(most * (1.0 / LEVELS), step_send.shape[1:])
        code_send[i] = jnp.round(value * (LEVELS / most)).astype(jnp.int32).astype(jnp.int16)
        return carry if early else send_out(i, carry)

    for h in range(halves):
        move_b(h).wait_recv()
        if h == halves - 1:
            lax.fori_loop(0, h * chunks, send_out, 0)
        lax.fori_loop(0, chunks, functools.partial(next_part, h, h < halves - 1), 0)

    for h in range(halves):

        def finish(c, carry, h=h):
            i = h * chunks + c
            move_step(i).wait_recv()
            move_code(i).wait_recv()
            code = code_recv[i].astype(jnp.int32).astype(jnp.float32)
            total = own_sum[piece(c), h * BLK:(h + 1) * BLK] + code * step_recv[i, 0:1, :]
            out_ref[piece(c), h * BLK:(h + 1) * BLK] = total.astype(out_ref.dtype)
            return carry

        lax.fori_loop(0, chunks, finish, 0)

    for h in range(halves):
        move_b(h).wait_send()

    def sent(i, carry):
        move_step(i).wait_send()
        move_code(i).wait_send()
        return carry

    lax.fori_loop(0, halves * chunks, sent, 0)


def hand_on(pieces, source, target, held, in_sem, out_sem):
    span = source.shape[0] // pieces

    def fetch(n):
        return pltpu.make_async_copy(source.at[n * span:(n + 1) * span, :], held.at[n], in_sem.at[n])

    def put(n):
        return pltpu.make_async_copy(held.at[n], target.at[n * span:(n + 1) * span, :], out_sem.at[n])

    for n in range(pieces):
        fetch(n).start()
    for n in range(pieces):
        fetch(n).wait()
        put(n).start()
    for n in range(pieces):
        put(n).wait()


def body(mat_a, mat_b, mask_a, mask_b):
    rows, inner = mat_a.shape
    width = mat_b.shape[1]
    block_rows = mask_a.shape[0]
    group = next(g for g in (4, 2, 1) if block_rows % g == 0)
    span = group * BLK
    chunks = rows // span
    halves = width // BLK
    sends = halves * chunks
    dma = pltpu.SemaphoreType.DMA
    product = pl.pallas_call(
        functools.partial(kernel, group),
        out_shape=jax.ShapeDtypeStruct((rows, width), jnp.bfloat16),
        in_specs=[
            pl.BlockSpec(memory_space=pl.ANY),
            pl.BlockSpec(memory_space=pl.ANY),
            pl.BlockSpec(memory_space=pltpu.SMEM),
            pl.BlockSpec(memory_space=pltpu.SMEM),
        ],
        out_specs=pl.BlockSpec(memory_space=pltpu.VMEM),
        scratch_shapes=[
            pltpu.VMEM((rows, inner), jnp.bfloat16),
            pltpu.VMEM((inner, width), jnp.bfloat16),
            pltpu.VMEM((inner, width), jnp.bfloat16),
            pltpu.VMEM((halves, inner, BLK), jnp.bfloat16),
            pltpu.VMEM((halves, inner, BLK), jnp.bfloat16),
            pltpu.VMEM((rows, width), jnp.float32),
            pltpu.VMEM((sends, span, BLK), jnp.int16),
            pltpu.VMEM((sends, span, BLK), jnp.int16),
            pltpu.VMEM((sends, 8, BLK), jnp.float32),
            pltpu.VMEM((sends, 8, BLK), jnp.float32),
            dma((chunks,)), dma((2,)), dma((halves,)), dma((halves,)),
            dma((sends,)), dma((sends,)), dma((sends,)), dma((sends,)),
        ],
        compiler_params=pltpu.CompilerParams(collective_id=0, has_side_effects=True),
        name="cannon",
    )(mat_a, mat_b, mask_a.T, mask_b.T)
    pieces = chunks
    return pl.pallas_call(
        functools.partial(hand_on, pieces),
        out_shape=jax.ShapeDtypeStruct(product.shape, product.dtype),
        in_specs=[pl.BlockSpec(memory_space=pl.ANY)],
        out_specs=pl.BlockSpec(memory_space=pl.ANY),
        scratch_shapes=[
            pltpu.VMEM((pieces, rows // pieces, width), product.dtype),
            dma((pieces,)), dma((pieces,)),
        ],
        name="hand_on",
    )(product)


def solution(mesh):
    return jax.shard_map(
        body,
        mesh=mesh,
        in_specs=(P("row", "col"), P("row", "col"), P("row", "col"), P("row", "col")),
        out_specs=P("row", "col"),
        check_vma=False,
    )
```
